32 devices in a mesh: grp: 2 (over y), chol: 4 (over z), orb: 4 (over x, core).
Axes of the slice: x: 2, y: 2, z: 4, core: 2. Of those that a mesh axis runs over, the one named last changes fastest.
Arguments:
- green: bfloat16 [32, 600, 896], P(('grp', 'chol'), None, 'orb'), parts along dimension 0, may hold values from -6 to 6
- half_chol: bfloat16 [80, 600, 896], P(('grp', 'chol'), None, 'orb'), parts along dimension 0, may hold values from -0.0078125 to 0.0078125
- chol_vec: bfloat16 [80, 896, 896], P(('grp', 'chol'), 'orb'), parts along dimension 0, may hold values from -0.0546875 to 0.0546875
- noise: float32 [32, 40], P('grp', 'chol'), parts along dimension 0, may hold values from -6 to 6
- order: int32 [32], P('grp'), parts along dimension 0, may hold values from 0 to 15, each once
- walkers: bfloat16 [32, 600, 896], P(('grp', 'chol'), None, 'orb'), parts along dimension 0, may hold values from -3 to 3
Outputs:
- force_bias: float32 [32, 40], P('grp', 'chol'), parts along dimension 0
- propagated: bfloat16 [32, 600, 896], P(('grp', 'chol'), None, 'orb'), parts along dimension 0
The draws below stay inside these ranges and needn't reach their ends.
There are 2 independent parts, one for each index of `grp`. The reference program is written for one: setup_inputs(seed, part) draws one part's arguments, and reference() takes and returns one part's arrays. A program takes and returns all parts, laid end to end along the dimension named above; each array names one. Nothing has to cross between parts.
Inputs may be any that keep to these rules, and one draw needn't show every extreme that they name: order is a permutation of the 16 walkers.
All inputs are finite; a program needn't handle non-finite values.
Results may differ from the reference program's by a relative error of at most 0.0086.
Values may be sent and summed in bfloat16 or wider, within the bound.
No kernel may reach another device: no remote copies, remote signals or barrier semaphores. Data moves between devices by JAX's collectives and lax.ppermute only.
A program may use at most 64 MiB of HBM per device.

```python
import jax
import jax.numpy as jnp

M = 896
NOCC = 600
W = 16
TERMS = 6
CHOL = 40


def steps_of(own_key, dims, shards, low, top_value):
    def one(position, blocks):
        draws = jax.random.uniform(jax.random.fold_in(jax.random.fold_in(own_key, 6), position), (blocks,), jnp.float32, low / len(shards), top_value / len(shards))
        return jnp.repeat(jnp.exp(draws), dims[position] // blocks).reshape((-1,) + (1,) * (len(dims) - position - 1))

    factor_of = one(*shards[0])
    for cut in shards[1:]:
        factor_of = factor_of * one(*cut)
    return factor_of


def normal_values(key, shape, scale, reach, pieces=(), kind=jnp.bfloat16):
    gain = steps_of(key, shape, pieces, -0.22, 0.18) if pieces else 1.0
    drawn = jax.random.normal(key, shape, jnp.float32) * scale * gain
    return jnp.minimum(jnp.maximum(drawn, -reach), reach).astype(kind)


def setup_inputs(seed: int = 0, part: int = 0) -> dict:
    arg_keys = jax.random.split(jax.random.key(seed), 7)
    part_splits = jax.random.split(jax.random.fold_in(arg_keys[6], part), 7)
    return {
        "green": normal_values(part_splits[0], (W, NOCC, M), 1.0, 6.0, ((0, 4), (2, 4))),
        "half_chol": normal_values(part_splits[1], (CHOL, NOCC, M), (NOCC * M) ** -0.5, 0.0078125, ((0, 4), (2, 4))),
        "chol_vec": normal_values(part_splits[2], (CHOL, M, M), (CHOL * M // 3) ** -0.5, 0.0546875, ((0, 4), (1, 4))),
        "noise": normal_values(part_splits[3], (W, CHOL), 1.0, 6.0, ((1, 4),), jnp.float32),
        "order": jax.random.permutation(part_splits[4], W).astype(jnp.int32),
        "walkers": normal_values(part_splits[5], (W, NOCC, M), 0.5, 3.0, ((0, 4), (2, 4))),
    }


def reference(green, half_chol, chol_vec, noise, order, walkers):
    chosen = jnp.take(green, order, axis=0)
    force_bias = jnp.dot(chosen.reshape(W, NOCC * M), half_chol.reshape(CHOL, NOCC * M).T, preferred_element_type=jnp.float32)
    fields = (noise - force_bias).astype(jnp.bfloat16)
    summed = jnp.dot(fields.astype(jnp.float32), chol_vec.reshape(CHOL, M * M).astype(jnp.float32), preferred_element_type=jnp.float32)
    propagator = summed.astype(jnp.bfloat16).reshape(W, M, M)
    prop_wide = propagator.astype(jnp.float32)
    running = walkers.astype(jnp.float32)
    term_now = walkers
    for power in range(1, TERMS + 1):
        scaled = jnp.einsum("wiq,wpq->wip", term_now.astype(jnp.float32), prop_wide, preferred_element_type=jnp.float32) / power
        running = running + scaled
        term_now = scaled.astype(jnp.bfloat16)
    return force_bias, running.astype(jnp.bfloat16)
```

```python
import functools

import jax
import jax.numpy as jnp
from jax import lax
from jax.experimental import pallas as pl
from jax.experimental.pallas import tpu as pltpu
from jax.sharding import PartitionSpec as P

TERMS = 6
LANE = 128
TILE = 16
PLANES = 4
VMEM_BYTES = 56 * 1024 * 1024
f32 = jnp.float32
bf16 = jnp.bfloat16

END = [(0, 1), (1, 0), (2, 3), (3, 2)]
MID = [(1, 2), (2, 1)]
CORE_SWAP = [(0, 1), (1, 0), (2, 3), (3, 2)]
CHIP_SWAP = [(0, 2), (2, 0), (1, 3), (3, 1)]


def plain_body(green, half_chol, chol_vec, noise, order, walkers):
    walk_dev = walkers.shape[0]
    all_green = lax.all_gather(green, "chol", axis=0, tiled=True)
    stored = lax.dot_general(
        all_green, half_chol, (((1, 2), (1, 2)), ((), ())), preferred_element_type=f32
    )
    stored = lax.psum(stored, "orb")
    force_bias = jnp.take(stored, order, axis=0)
    fields = (noise - force_bias).astype(bf16)
    flat_chol = chol_vec.reshape(chol_vec.shape[0], -1)
    summed = lax.psum_scatter(
        jnp.dot(fields, flat_chol, preferred_element_type=f32),
        "chol",
        scatter_dimension=0,
        tiled=True,
    )
    propagator = summed.astype(bf16).reshape(walk_dev, chol_vec.shape[1], chol_vec.shape[2])
    full_prop = lax.all_gather(propagator, "orb", axis=1, tiled=True)
    column_walkers = lax.all_to_all(walkers, "orb", split_axis=1, concat_axis=2, tiled=True)
    running = column_walkers.astype(f32)
    term_now = column_walkers
    for power in range(1, TERMS + 1):
        scaled = jnp.einsum("wiq,wpq->wip", term_now, full_prop, preferred_element_type=f32) / power
        running = running + scaled
        term_now = scaled.astype(bf16)
    propagated = lax.all_to_all(
        running.astype(bf16), "orb", split_axis=2, concat_axis=1, tiled=True
    )
    return force_bias, propagated


def spec_vmem():
    return pl.BlockSpec(memory_space=pltpu.VMEM)


def spec_smem():
    return pl.BlockSpec(memory_space=pltpu.SMEM)


def pack(x):
    n, r, c = x.shape
    tiles = pl.cdiv(c, LANE)

    def kernel(x_ref, o_ref):
        for t in range(tiles):
            width = min(LANE, c - t * LANE)
            if width < LANE:
                o_ref[0, t] = jnp.zeros((r, LANE), x.dtype)
            o_ref[0, t, :, :width] = x_ref[0, :, t * LANE : t * LANE + width]

    return pl.pallas_call(
        kernel,
        out_shape=jax.ShapeDtypeStruct((n, tiles, r, LANE), x.dtype),
        grid=(n,),
        in_specs=[pl.BlockSpec((1, r, c), lambda i: (i, 0, 0))],
        out_specs=pl.BlockSpec((1, tiles, r, LANE), lambda i: (i, 0, 0, 0)),
        cost_estimate=pl.CostEstimate(flops=0, bytes_accessed=4 * x.size, transcendentals=0),
        name="pack",
    )(x)


def xor_order(x, orb):
    n, r, c = x.shape

    def kernel(orb_ref, x_ref, o_ref):
        o_ref[...] = x_ref[...]

    return pl.pallas_call(
        kernel,
        out_shape=jax.ShapeDtypeStruct(x.shape, x.dtype),
        grid_spec=pltpu.PrefetchScalarGridSpec(
            num_scalar_prefetch=1,
            grid=(n,),
            in_specs=[pl.BlockSpec((1, r, c), lambda i, o: (i ^ o[0], 0, 0))],
            out_specs=pl.BlockSpec((1, r, c), lambda i, o: (i, 0, 0)),
        ),
        cost_estimate=pl.CostEstimate(flops=0, bytes_accessed=4 * x.size, transcendentals=0),
        name="xor_order",
    )(orb, x)


def xor_exchange(blocks):
    across = lax.ppermute(blocks[2:4], "orb", CHIP_SWAP)
    beside = lax.ppermute(jnp.concatenate([blocks[1:2], across[1:2]]), "orb", CORE_SWAP)
    return blocks[0:1], beside[0:1], across[0:1], beside[1:2]


def prop_rows(place, fields, own, near, own_at, near_at, rows, far, recv):
    vecs, _, cols = own.shape
    packed = near.ndim == 4
    walk_all = fields.shape[0]
    walk_dev = walk_all // PLANES
    walk_out = 2 * walk_dev
    wide = vecs * TILE
    lane_tiles = cols // LANE

    def expand(place_ref, f_ref, x_scr):
        chol, orb = place_ref[0], place_ref[1]
        half = chol // 2
        row = lax.broadcasted_iota(jnp.int32, (walk_out * TILE, walk_all), 0) // TILE
        col = lax.broadcasted_iota(jnp.int32, (walk_out * TILE, walk_all), 1)
        side = (1 - half) if far else half
        plane = jnp.where(row < walk_dev, side * (PLANES - 1), side + 1)
        want = plane * walk_dev + ((row % walk_dev) ^ orb)
        pick = (want == col).astype(bf16)
        by_row = jnp.dot(pick, f_ref[...], preferred_element_type=f32).astype(bf16)
        vec = lax.broadcasted_iota(jnp.int32, (2 * vecs, 2 * wide), 0)
        col2 = lax.broadcasted_iota(jnp.int32, (2 * vecs, 2 * wide), 1) // TILE
        spread = (vec == col2).astype(bf16)
        full = jnp.dot(by_row, spread, preferred_element_type=f32)
        r = lax.broadcasted_iota(jnp.int32, (walk_out * TILE, 2 * wide), 0) % TILE
        c = lax.broadcasted_iota(jnp.int32, (walk_out * TILE, 2 * wide), 1) % TILE
        x_scr[...] = jnp.where(r == c, full, 0.0).astype(bf16)

    def kernel(place_ref, f_ref, own_ref, near_ref, *rest):
        if recv is None:
            o_ref, x_scr = rest
        else:
            recv_ref, o_ref, x_scr = rest

        @pl.when(pl.program_id(0) == 0)
        def _():
            expand(place_ref, f_ref, x_scr)

        x_own = x_scr[:, :wide]
        x_near = x_scr[:, wide:]
        for t in range(0, lane_tiles):
            at = slice(t * LANE, (t + 1) * LANE)
            mine = own_ref[:, :, at].reshape(wide, LANE)
            other = (near_ref[:, t] if packed else near_ref[:, :, at]).reshape(wide, LANE)
            total = jnp.dot(x_own, mine, preferred_element_type=f32)
            total = total + jnp.dot(x_near, other, preferred_element_type=f32)
            total = total.reshape(walk_out, TILE, LANE)
            if recv is not None:
                total = total + recv_ref[:, :, at].astype(f32)
            o_ref[:, :, at] = total.astype(bf16)

    if packed:
        near_spec = pl.BlockSpec(
            (vecs, lane_tiles, TILE, LANE), lambda i, p: (0, 0, near_at // TILE + i, 0)
        )
    else:
        near_spec = pl.BlockSpec((vecs, TILE, cols), lambda i, p: (0, near_at // TILE + i, 0))
    in_specs = [
        pl.BlockSpec(fields.shape, lambda i, p: (0, 0)),
        pl.BlockSpec((vecs, TILE, cols), lambda i, p: (0, own_at // TILE + i, 0)),
        near_spec,
    ]
    args = [fields, own, near]
    block = pl.BlockSpec((walk_out, TILE, cols), lambda i, p: (0, i, 0))
    if recv is not None:
        in_specs.append(block)
        args.append(recv)
    size = walk_out * rows * cols
    return pl.pallas_call(
        kernel,
        out_shape=jax.ShapeDtypeStruct((walk_out, rows, cols), bf16),
        grid_spec=pltpu.PrefetchScalarGridSpec(
            num_scalar_prefetch=1,
            grid=(rows // TILE,),
            in_specs=in_specs,
            out_specs=block,
            scratch_shapes=[pltpu.VMEM((walk_out * TILE, 2 * wide), bf16)],
        ),
        cost_estimate=pl.CostEstimate(
            flops=2 * size * 2 * vecs * TILE, bytes_accessed=2 * size, transcendentals=0
        ),
        name="prop_far" if far else "prop_near",
    )(place, *args)


def taylor(place, prop, starts, walk):
    q_all = prop[0][0].shape[2]
    block, occ = walk[0].shape[1:]
    flat = [piece for chunk in prop for piece in chunk]
    n_prop = len(flat)

    def kernel(place_ref, *refs):
        prop_refs = refs[:n_prop]
        walk_refs = refs[n_prop : n_prop + 4]
        o_ref, p_scr, t_a, t_b, run = refs[n_prop + 4 :]
        orb = place_ref[1]
        for d in range(4):
            at = pl.multiple_of((orb ^ d) * block, TILE)
            start = walk_refs[d][0]
            t_a[pl.ds(at, block), :] = start
            run[pl.ds(at, block), :] = start.astype(f32)
            for n, first in enumerate(starts):
                piece = prop_refs[4 * n + d]
                p_scr[pl.ds(pl.multiple_of(at + first, TILE), piece.shape[1]), :] = piece[0]
        for power in range(1, TERMS + 1):
            src, dst = (t_a, t_b) if power % 2 else (t_b, t_a)
            scale = 1.0 / power

            def rows(n, _, src=src, dst=dst, scale=scale):
                at = pl.ds(pl.multiple_of(n * block, TILE), block)
                term = jnp.dot(p_scr[at, :], src[...], preferred_element_type=f32) * scale
                run[at, :] += term
                dst[at, :] = term.astype(bf16)
                return 0

            lax.fori_loop(0, 4, rows, 0)
        for d in range(4):
            at = pl.multiple_of((orb ^ d) * block, TILE)
            o_ref[d] = run[pl.ds(at, block), :].astype(bf16)

    return pl.pallas_call(
        kernel,
        out_shape=jax.ShapeDtypeStruct((4, block, occ), bf16),
        in_specs=[spec_smem()] + [spec_vmem()] * (n_prop + 4),
        out_specs=spec_vmem(),
        scratch_shapes=[
            pltpu.VMEM((q_all, q_all), bf16),
            pltpu.VMEM((q_all, occ), bf16),
            pltpu.VMEM((q_all, occ), bf16),
            pltpu.VMEM((q_all, occ), f32),
        ],
        compiler_params=pltpu.CompilerParams(vmem_limit_bytes=VMEM_BYTES),
        cost_estimate=pl.CostEstimate(
            flops=2 * TERMS * q_all * q_all * occ, bytes_accessed=8 * q_all * occ, transcendentals=0
        ),
        name="taylor",
    )(place, *flat, *walk)


def line_body(green, half_chol, chol_vec, noise, order, walkers):
    chol = lax.axis_index("chol")
    orb = lax.axis_index("orb")
    outer = (chol == 0) | (chol == PLANES - 1)
    place = jnp.stack([chol, orb]).astype(jnp.int32)
    walk_dev = walkers.shape[0]
    vecs, rows, cols = chol_vec.shape
    walk_all = noise.shape[0]

    walk_t = xor_order(walkers.transpose(0, 2, 1), place[1:])
    walk_in = xor_exchange(walk_t)

    own_g = pack(green.transpose(0, 2, 1))
    packed_h = pack(half_chol.transpose(0, 2, 1))
    unit = own_g.size // (vecs * cols) // TILE * TILE
    chunk_rows = [unit, unit, unit, rows - 3 * unit]
    chunk_at = [0, unit, 2 * unit, 3 * unit]

    def chol_part(n):
        part = pack(chol_vec[:, chunk_at[n] : chunk_at[n] + chunk_rows[n], :])
        return part.reshape(own_g.shape)

    def as_part(x):
        return x.reshape(vecs, cols // LANE, unit, LANE)

    def contract(x):
        return lax.dot_general(
            x, packed_h, (((1, 2, 3), (1, 2, 3)), ((), ())), preferred_element_type=f32
        )

    end1 = lax.ppermute(own_g, "chol", END)
    mid1 = lax.ppermute(own_g, "chol", MID)
    noise_near = lax.ppermute(noise, "chol", END)
    part0, part1 = chol_part(0), chol_part(1)
    end1, mid1 = lax.optimization_barrier((end1, mid1))
    end2 = lax.ppermute(jnp.where(outer, part0, mid1), "chol", END)
    mid2 = lax.ppermute(end1, "chol", MID)
    dot_own, dot_1, dot_m1 = contract(own_g), contract(end1), contract(mid1)
    end2, mid2 = lax.optimization_barrier((end2, mid2))
    end3 = lax.ppermute(jnp.where(outer, part1, mid2), "chol", END)
    dot_e2, dot_m2 = contract(end2), contract(mid2)
    dot_e3 = contract(end3)
    stored = jnp.concatenate(
        [dot_own, dot_1, jnp.where(outer, dot_e2, dot_m1), jnp.where(outer, dot_e3, dot_m2)]
    )
    gap = (order // walk_dev) ^ chol
    slot = jnp.where((gap >= 2) & ~outer, 5 - gap, gap)
    at = slot * walk_dev + order % walk_dev
    hot = at[:, None] == jnp.arange(walk_all)[None, :]
    bias_part = jnp.sum(jnp.where(hot[:, :, None], stored[None], 0.0), axis=1)
    near_part = lax.ppermute(bias_part, "chol", END)
    both = jnp.concatenate([bias_part, near_part], axis=1)
    both = both + lax.ppermute(both, "orb", CORE_SWAP)
    both = both + lax.ppermute(both, "orb", CHIP_SWAP)
    force_bias = both[:, :vecs]
    fields = (jnp.concatenate([noise, noise_near], axis=1) - both).astype(bf16)

    rest_in, end3, _ = lax.optimization_barrier((chol_vec[:, 2 * unit :, :], end3, near_part))
    rest = lax.ppermute(rest_in, "chol", END)
    near = [as_part(end2), as_part(end3), rest, rest]
    near_at = [0, 0, 0, unit]

    prop_pieces = []
    came = []
    for n in range(4):
        args = (place, fields, chol_vec, near[n], chunk_at[n], near_at[n], chunk_rows[n])
        far = prop_rows(*args, True, None)
        if n >= 2:
            far, came[n - 2] = lax.optimization_barrier((far, came[n - 2]))
        came.append(lax.ppermute(far, "chol", MID))
    for n in range(4):
        args = (place, fields, chol_vec, near[n], chunk_at[n], near_at[n], chunk_rows[n])
        done = prop_rows(*args, False, came[n])
        handed = lax.ppermute(done[:walk_dev], "chol", END)
        mine = jnp.where(outer, handed, done[walk_dev:])
        prop_pieces.append(xor_exchange(mine))

    out_blocks = taylor(place, prop_pieces, chunk_at, walk_in)
    back = jnp.concatenate(xor_exchange(out_blocks))
    propagated = xor_order(back, place[1:]).transpose(0, 2, 1)
    return force_bias, propagated


def solution(mesh):
    def body(green, half_chol, chol_vec, noise, order, walkers):
        fits = (
            mesh.shape["chol"] == PLANES
            and mesh.shape["orb"] == 4
            and walkers.shape[0] == 4
            and chol_vec.shape[1] % TILE == 0
            and chol_vec.shape[2] % LANE == 0
        )
        if fits:
            tiles = pl.cdiv(green.shape[1], LANE) * LANE * green.shape[0] * green.shape[2]
            unit = tiles // (chol_vec.shape[0] * chol_vec.shape[2])
            fits = (
                unit * chol_vec.shape[0] * chol_vec.shape[2] == tiles
                and unit % TILE == 0
                and 0 < chol_vec.shape[1] - 3 * unit
            )
        chosen = line_body if fits else plain_body
        return chosen(green, half_chol, chol_vec, noise, order, walkers)

    return jax.shard_map(
        body,
        mesh=mesh,
        in_specs=(
            P(("grp", "chol"), None, "orb"),
            P(("grp", "chol"), None, "orb"),
            P(("grp", "chol"), "orb", None),
            P("grp", "chol"),
            P("grp"),
            P(("grp", "chol"), None, "orb"),
        ),
        out_specs=(P("grp", "chol"), P(("grp", "chol"), None, "orb")),
        check_vma=False,
    )
```
